32 devices in a mesh: seq: 8 (over z, y), chan: 4 (over x, core).
Axes of the slice: x: 2, y: 2, z: 4, core: 2. Of those that a mesh axis runs over, the one named last changes fastest.
Arguments:
- q_proj: bfloat16 [2048, 2048], P('seq', 'chan'), parts along dimension 1, may hold values from -6 to 6
- k_proj: bfloat16 [2048, 2048], P('seq', 'chan'), parts along dimension 1, may hold values from -6 to 6
- v_proj: bfloat16 [2048, 2048], P('seq', 'chan'), parts along dimension 1, may hold values from -6 to 6
- filter_spectrum: float32 [2, 16, 256, 2048], P(None, 'seq', None, 'chan'), parts along dimension 3, may hold values from -6 to 6
- skip: float32 [2048], P('chan'), parts along dimension 0, may hold values from 0.1 to 1.9
Outputs:
- mixed: bfloat16 [2048, 2048], P('seq', 'chan'), parts along dimension 1
The draws below stay inside these ranges and needn't reach their ends.
There are 4 independent parts, one for each index of `chan`. The reference program is written for one: setup_inputs(seed, part) draws one part's arguments, and reference() takes and returns one part's arrays. A program takes and returns all parts, laid end to end along the dimension named above; each array names one. Nothing has to cross between parts.
All inputs are finite; a program needn't handle non-finite values.
Results may differ from the reference program's by a relative error of at most 0.0063.
Values may be sent and summed in bfloat16 or wider, within the bound.
No kernel may reach another device: no remote copies, remote signals or barrier semaphores. Data moves between devices by JAX's collectives and lax.ppermute only.
A program may use at most 64 MiB of HBM per device.

```python
import jax
import jax.numpy as jnp

C = 512
TOK_DEV = 256
L = 2048
P_SIZE = 16


def levels(rng, dims, shards, low, high):
    level, own = 1.0, jax.random.fold_in(rng, 6)
    for dim, blocks in shards:
        steps = jnp.exp(jax.random.uniform(jax.random.fold_in(own, dim), (blocks,), jnp.float32, low / len(shards), high / len(shards)))
        level = level * jnp.repeat(steps, dims[dim] // blocks).reshape([-1 if axis == dim else 1 for axis in range(len(dims))])
    return level


def scatter_about(rng, dims, spread, most, shards=(), held_as=jnp.bfloat16):
    result = jax.random.normal(rng, dims, jnp.float32) * spread
    if len(shards) > 0:
        result = levels(rng, dims, shards, -0.22, 0.18) * result
    return jnp.clip(result, min=-most, max=most).astype(held_as)


def setup_inputs(seed: int = 0, part: int = 0) -> dict:
    key_list = jax.random.split(jax.random.key(seed), 6)
    part_keys = jax.random.split(jax.random.fold_in(key_list[5], part), 6)
    q_proj = scatter_about(part_keys[0], (L, C), 1.0, 6.0, ((0, 8),))
    k_proj = scatter_about(part_keys[1], (L, C), 1.0, 6.0, ((0, 8),))
    v_proj = scatter_about(part_keys[2], (L, C), 1.0, 6.0, ((0, 8),))
    filter_spectrum = scatter_about(part_keys[3], (2, P_SIZE, TOK_DEV, C), 1.0, 6.0, ((1, 8),), jnp.float32)
    skip = jnp.clip(1.0 + 0.18 * jax.random.normal(part_keys[4], (C,), jnp.float32), 0.1, 1.9)
    return dict(q_proj=q_proj, k_proj=k_proj, v_proj=v_proj, filter_spectrum=filter_spectrum, skip=skip)


def dft_table(length):
    index = jnp.arange(length, dtype=jnp.int32)
    product = (index[:, None] * index[None, :]) % length
    angle = (2.0 * jnp.pi / length) * product.astype(jnp.float32)
    return jnp.cos(angle).astype(jnp.bfloat16), jnp.sin(angle).astype(jnp.bfloat16)


def twiddle(freq_count, column_count, points):
    freqs = jnp.arange(freq_count, dtype=jnp.int32)
    columns = jnp.arange(column_count, dtype=jnp.int32)
    product = (freqs[:, None] * columns[None, :]) % points
    angle = (2.0 * jnp.pi / points) * product.astype(jnp.float32)
    return jnp.cos(angle)[:, :, None], jnp.sin(angle)[:, :, None]


def mix_inner(table, values, form):
    return jnp.einsum(form, table.astype(jnp.float32), values.astype(jnp.float32))


def reference(q_proj, k_proj, v_proj, filter_spectrum, skip):
    points = P_SIZE * TOK_DEV
    halves = P_SIZE // 2
    gated = (k_proj.astype(jnp.float32) * v_proj.astype(jnp.float32)).astype(jnp.bfloat16)
    outer_cos, outer_sin = dft_table(P_SIZE)
    inner_cos, inner_sin = dft_table(TOK_DEV)
    turn_cos, turn_sin = twiddle(P_SIZE, TOK_DEV, points)
    flattened = gated.reshape(halves, TOK_DEV * C)
    raw_real = jnp.dot(outer_cos[:, :halves], flattened, preferred_element_type=jnp.float32).reshape(P_SIZE, TOK_DEV, C)
    raw_imag = -jnp.dot(outer_sin[:, :halves], flattened, preferred_element_type=jnp.float32).reshape(P_SIZE, TOK_DEV, C)
    first_real = (raw_real * turn_cos + raw_imag * turn_sin).astype(jnp.bfloat16)
    first_imag = (raw_imag * turn_cos - raw_real * turn_sin).astype(jnp.bfloat16)
    forward = "gn,anc->agc"
    spec_real = mix_inner(inner_cos, first_real, forward) + mix_inner(inner_sin, first_imag, forward)
    spec_imag = mix_inner(inner_cos, first_imag, forward) - mix_inner(inner_sin, first_real, forward)
    filt_real = filter_spectrum[0]
    filt_imag = filter_spectrum[1]
    prod_real = (spec_real * filt_real - spec_imag * filt_imag).astype(jnp.bfloat16)
    prod_imag = (spec_real * filt_imag + spec_imag * filt_real).astype(jnp.bfloat16)
    inverse = "ng,agc->anc"
    mid_real = mix_inner(inner_cos, prod_real, inverse) - mix_inner(inner_sin, prod_imag, inverse)
    mid_imag = mix_inner(inner_cos, prod_imag, inverse) + mix_inner(inner_sin, prod_real, inverse)
    back_real = (mid_real * turn_cos - mid_imag * turn_sin).astype(jnp.bfloat16)
    back_imag = (mid_imag * turn_cos + mid_real * turn_sin).astype(jnp.bfloat16)
    conv = jnp.dot(outer_cos[:halves], back_real.reshape(P_SIZE, TOK_DEV * C), preferred_element_type=jnp.float32)
    conv = conv - jnp.dot(outer_sin[:halves], back_imag.reshape(P_SIZE, TOK_DEV * C), preferred_element_type=jnp.float32)
    conv = conv.reshape(halves * TOK_DEV, C) / points
    mixed = q_proj.astype(jnp.float32) * (conv + skip[None, :] * gated.astype(jnp.float32))
    return mixed.astype(jnp.bfloat16)
```

```python
import functools

import jax
import jax.numpy as jnp
import numpy as np
from jax import lax
from jax.experimental import pallas as pl
from jax.experimental.pallas import tpu as pltpu
from jax.sharding import PartitionSpec as P

LANES = 128
GROUP = 16
ANY = pl.BlockSpec(memory_space=pl.ANY)
VMEM = pl.BlockSpec(memory_space=pltpu.VMEM)


def dft_table(length):
    index = np.arange(length, dtype=np.int64)
    product = index[:, None] * index[None, :] % length
    angle = np.float32(2.0 * np.pi / length) * product.astype(np.float32)
    return np.cos(angle).astype(jnp.bfloat16), np.sin(angle).astype(jnp.bfloat16)


def device_tables(devices, block, tokens, me):
    points = 2 * devices * tokens
    xor = np.arange(devices)[:, None] ^ np.arange(devices)[None, :]
    freqs = (2 * xor[:, :block, None] + np.arange(2)).reshape(devices, 2 * block)
    cos, sin = dft_table(2 * devices)
    pairs = np.stack([cos, -sin], axis=1)[freqs[:, :, None, None], np.arange(2)[:, None], xor[:, None, None, :]]
    product = np.arange(2 * devices)[:, None] * np.arange(tokens)[None, :] % points
    angle = np.float32(2.0 * np.pi / points) * product.astype(np.float32)
    turn = np.stack([np.cos(angle), np.sin(angle)], axis=1)[freqs].reshape(devices, 4 * block, tokens)
    pairs = pairs.reshape(devices, 4 * block, devices)
    eye = np.eye(GROUP, dtype=np.float32).astype(jnp.bfloat16)
    if devices > 8:
        pairs = lax.dynamic_index_in_dim(jnp.asarray(pairs), me, 0, True)
        turn = lax.dynamic_index_in_dim(jnp.asarray(turn), me, 0, True)
        eye = jnp.asarray(eye)
    outer = pairs[:, :, None, :, None] * eye[None, None, :, None, :]
    return outer.reshape(outer.shape[0], 4 * block * GROUP, devices * GROUP), turn


def inner_table(tokens):
    cos, sin = dft_table(tokens)
    return np.concatenate([cos, sin, cos, -sin, cos], axis=1)


def split_kernel(block, k_ref, v_ref, filt_ref, *outs):
    member = lax.rem(lax.axis_index("seq"), block)
    for mask in range(block):
        lanes = pl.ds(pl.multiple_of((member ^ mask) * LANES, LANES), LANES)
        gated = k_ref[:, lanes].astype(jnp.float32) * v_ref[:, lanes].astype(jnp.float32)
        outs[mask][...] = gated.astype(jnp.bfloat16)
        outs[block + mask][...] = filt_ref[:, :, :, lanes].astype(jnp.bfloat16)


def transform_kernel(devices, block, tokens, *refs):
    gated, filt = refs[:devices], refs[devices : devices + block]
    outer_in, outer_back_in, turn_in, inner_ref = refs[devices + block : devices + block + 4]
    outs = refs[devices + block + 4 : 2 * devices + block + 4]
    outer, outer_back, turn_rows, turn, first, back, sem = refs[2 * devices + block + 4 :]
    mine = lax.rem(lax.axis_index("seq"), outer_in.shape[0])
    groups = tokens // GROUP
    copies = [
        pltpu.make_async_copy(turn_in.at[mine], turn_rows, sem.at[0]),
        pltpu.make_async_copy(outer_in.at[mine], outer, sem.at[1]),
        pltpu.make_async_copy(outer_back_in.at[mine], outer_back, sem.at[2]),
    ]
    for copy in copies:
        copy.start()
    for copy in copies:
        copy.wait()
    turn[...] = turn_rows[...].T
    for g in range(0, groups, 2):
        rows = [pl.ds((g + h) * GROUP, GROUP) for h in range(2)]
        data = [jnp.concatenate([part[r, :] for part in gated], axis=0) for r in rows]
        raw = jnp.dot(outer[...], jnp.concatenate(data, axis=1), preferred_element_type=jnp.float32)
        for m in range(block):
            for h in range(2):
                for f in range(2):
                    at = (2 * m + f) * 2
                    cos, sin = turn[rows[h], at : at + 1], turn[rows[h], at + 1 : at + 2]
                    lanes = slice(h * LANES, (h + 1) * LANES)
                    at = at * GROUP
                    real, imag = raw[at : at + GROUP, lanes], raw[at + GROUP : at + 2 * GROUP, lanes]
                    out = pl.ds(f * LANES, LANES)
                    first[m, rows[h], out] = (real * cos + imag * sin).astype(jnp.bfloat16)
                    first[m, pl.ds(tokens + (g + h) * GROUP, GROUP), out] = (imag * cos - real * sin).astype(jnp.bfloat16)
    for m in range(block):
        values = first[m]
        spec_real = jnp.dot(inner_ref[:, : 2 * tokens], values, preferred_element_type=jnp.float32)
        spec_imag = jnp.dot(inner_ref[:, 3 * tokens :], values, preferred_element_type=jnp.float32)
        filt_real = jnp.concatenate([filt[m][0, f] for f in range(2)], axis=1).astype(jnp.float32)
        filt_imag = jnp.concatenate([filt[m][1, f] for f in range(2)], axis=1).astype(jnp.float32)
        prod_real = (spec_real * filt_real - spec_imag * filt_imag).astype(jnp.bfloat16)
        prod_imag = (spec_real * filt_imag + spec_imag * filt_real).astype(jnp.bfloat16)
        product = jnp.concatenate([prod_real, prod_imag], axis=0)
        mid_real = jnp.dot(inner_ref[:, 2 * tokens : 4 * tokens], product, preferred_element_type=jnp.float32)
        mid_imag = jnp.dot(inner_ref[:, tokens : 3 * tokens], product, preferred_element_type=jnp.float32)
        for f in range(2):
            lanes = slice(f * LANES, (f + 1) * LANES)
            at = (2 * m + f) * 2
            cos, sin = turn[:, at : at + 1], turn[:, at + 1 : at + 2]
            real = (mid_real[:, lanes] * cos - mid_imag[:, lanes] * sin).astype(jnp.bfloat16)
            imag = (mid_imag[:, lanes] * cos + mid_real[:, lanes] * sin).astype(jnp.bfloat16)
            back[:, at] = real.reshape(groups, GROUP, LANES)
            back[:, at + 1] = imag.reshape(groups, GROUP, LANES)
    scale = 1.0 / (2 * devices * tokens)
    for g in range(0, groups, 2):
        data = jnp.concatenate([back[g + h].reshape(4 * block * GROUP, LANES) for h in range(2)], axis=1)
        part = (jnp.dot(outer_back[...], data, preferred_element_type=jnp.float32) * scale).astype(jnp.bfloat16)
        for h in range(2):
            for j in range(devices):
                outs[j][pl.ds((g + h) * GROUP, GROUP), :] = part[j * GROUP : (j + 1) * GROUP, h * LANES : (h + 1) * LANES]


def gate_kernel(devices, block, q_ref, k_ref, v_ref, skip_ref, *refs):
    parts, out_ref = refs[:devices], refs[devices]
    member = lax.rem(lax.axis_index("seq"), block)
    for m in range(block):
        lanes = pl.ds(pl.multiple_of((member ^ m) * LANES, LANES), LANES)
        conv = parts[m][...].astype(jnp.float32)
        for other in range(m + block, devices, block):
            conv = conv + parts[other][...].astype(jnp.float32)
        gated = (k_ref[:, lanes].astype(jnp.float32) * v_ref[:, lanes].astype(jnp.float32)).astype(jnp.bfloat16)
        mixed = q_ref[:, lanes].astype(jnp.float32) * (conv + skip_ref[:, lanes] * gated.astype(jnp.float32))
        out_ref[:, lanes] = mixed.astype(jnp.bfloat16)


def body(q_proj, k_proj, v_proj, filter_spectrum, skip):
    devices = lax.axis_size("seq")
    tokens, channels = q_proj.shape
    block = min(devices, channels // LANES)
    params = pltpu.CompilerParams(vmem_limit_bytes=32 * 1024 * 1024)
    piece = jax.ShapeDtypeStruct((tokens, LANES), jnp.bfloat16)
    filt_shape = filter_spectrum.shape[:3] + (LANES,)
    filt_piece = jax.ShapeDtypeStruct(filt_shape, jnp.bfloat16)

    def swap(value, mask):
        return lax.ppermute(value, "seq", [(i, i ^ mask) for i in range(devices)])

    pieces = pl.pallas_call(
        functools.partial(split_kernel, block),
        out_shape=[piece] * block + [filt_piece] * block,
        in_specs=[VMEM] * 3,
        out_specs=[VMEM] * (2 * block),
        compiler_params=params,
        name="split",
    )(k_proj, v_proj, filter_spectrum)
    gated, filt = pieces[:block], pieces[block:]
    filt_all = [filt[0]] + [swap(filt[m], m) for m in range(1, block)]
    gated_all = [gated[0]] + [swap(gated[m % block], m) for m in range(1, devices)]
    outer, turn = device_tables(devices, block, tokens, lax.axis_index("seq"))
    parts = pl.pallas_call(
        functools.partial(transform_kernel, devices, block, tokens),
        out_shape=[piece] * devices,
        in_specs=[VMEM] * (devices + block) + [ANY] * 3 + [VMEM],
        out_specs=[VMEM] * devices,
        scratch_shapes=[
            pltpu.VMEM(outer.shape[1:], jnp.bfloat16),
            pltpu.VMEM(outer.shape[:0:-1], jnp.bfloat16),
            pltpu.VMEM(turn.shape[1:], jnp.float32),
            pltpu.VMEM(turn.shape[:0:-1], jnp.float32),
            pltpu.VMEM((block, 2 * tokens, 2 * LANES), jnp.bfloat16),
            pltpu.VMEM((tokens // GROUP, 4 * block, GROUP, LANES), jnp.bfloat16),
            pltpu.SemaphoreType.DMA((3,)),
        ],
        compiler_params=params,
        name="transform",
    )(
        *gated_all,
        *filt_all,
        jnp.asarray(outer),
        jnp.asarray(outer.transpose(0, 2, 1)),
        jnp.asarray(turn),
        jnp.asarray(inner_table(tokens)),
    )
    arrived = [parts[0]] + [swap(parts[m], m) for m in range(1, devices)]
    return pl.pallas_call(
        functools.partial(gate_kernel, devices, block),
        out_shape=jax.ShapeDtypeStruct((tokens, channels), jnp.bfloat16),
        in_specs=[VMEM] * (4 + devices),
        out_specs=VMEM,
        compiler_params=params,
        name="gate",
    )(q_proj, k_proj, v_proj, skip[None, :], *arrived)


def solution(mesh):
    in_specs = (
        P("seq", "chan"),
        P("seq", "chan"),
        P("seq", "chan"),
        P(None, "seq", None, "chan"),
        P("chan"),
    )
    out_specs = P("seq", "chan")
    return jax.shard_map(body, mesh=mesh, in_specs=in_specs, out_specs=out_specs, check_vma=False)
```
